128 devices in a mesh: seq: 32 (over z, y, core), ch: 4 (over x).
Axes of the slice: x: 4, y: 4, z: 4, core: 2. Of those that a mesh axis runs over, the one named last changes fastest.
Arguments:
- query_proj: bfloat16 [16384, 512], P('seq', 'ch'), may hold values from -6 to 6
- key_proj: bfloat16 [16384, 512], P('seq', 'ch'), may hold values from -6 to 6
- value_proj: bfloat16 [16384, 512], P('seq', 'ch'), may hold values from -6 to 6
- filter_taps: float32 [16384, 128], P('seq'), may hold values from -1.1 to 1.1, as said below
- skip_gain: float32 [512], P('ch'), may hold values from 0.3 to 3
- grad_mixer: bfloat16 [16384, 512], P('seq', 'ch'), may hold values from -6 to 6
Outputs:
- mixer_out: bfloat16 [16384, 512], P('seq', 'ch')
- grad_query: bfloat16 [16384, 512], P('seq', 'ch')
- grad_key: bfloat16 [16384, 512], P('seq', 'ch')
- grad_value: bfloat16 [16384, 512], P('seq', 'ch')
- grad_filter: float32 [16384, 128], P('seq', 'ch')
The draws below stay inside these ranges and needn't reach their ends.
Inputs may be any that keep to these rules, and one draw needn't show every extreme that they name: `filter_taps`: real-valued filter taps.
All inputs are finite; a program needn't handle non-finite values.
Results may differ from the reference program's by a relative error of at most 0.001.
Values sent between devices are 32-bit elements; how exact they have to be, the bound alone decides.
No kernel may reach another device: no remote copies, remote signals or barrier semaphores. Data moves between devices by JAX's collectives and lax.ppermute only.
A program may use at most 64 MiB of HBM per device.

```python
import math
import jax
import jax.numpy as jnp

CH = 512
KERNEL_GROUPS = 128
SEQUENCE_STEPS = 16384


def draw_filter_taps(key, part):
    seed_jitter_samples, seed_extent, seed_spike_samples, seed_masking = jax.random.split(key, 4)
    delay_shifts = jnp.arange(SEQUENCE_STEPS, dtype=jnp.float32)[:, None]
    low_log = math.log(30.0)
    high_log = math.log(4.0 * SEQUENCE_STEPS)
    noise = jax.random.truncated_normal(seed_jitter_samples, -4.0, 4.0, (SEQUENCE_STEPS, KERNEL_GROUPS), jnp.float32)
    reach = jnp.exp(jax.random.uniform(seed_extent, (1, KERNEL_GROUPS), jnp.float32, low_log, high_log))
    decay = jnp.exp(-delay_shifts / reach)
    spike_occurrences = jax.random.randint(seed_spike_samples, (3, 1, KERNEL_GROUPS), 1, SEQUENCE_STEPS).astype(jnp.float32)
    successful_tests = jnp.sum((delay_shifts[None, :, :] >= spike_occurrences).astype(jnp.float32), axis=0)
    keep = jax.random.uniform(seed_masking, (1, KERNEL_GROUPS), jnp.float32, 0.5, 0.8)
    norm_factor = jnp.sqrt(2.0 / (reach * (1.0 - jnp.exp(-2.0 * SEQUENCE_STEPS / reach))))
    return (noise * decay * keep ** successful_tests * norm_factor).astype(jnp.float32)


def level_of(stream_key, shape, cuts, least, top_value):
    loudness, own = 1.0, jax.random.fold_in(stream_key, 6)
    for position, blocks in cuts:
        steps = jnp.exp(jax.random.uniform(jax.random.fold_in(own, position), (blocks,), jnp.float32, least / len(cuts), top_value / len(cuts)))
        loudness = loudness * jnp.repeat(steps, shape[position] // blocks).reshape([-1 if axis == position else 1 for axis in range(len(shape))])
    return loudness


def scatter_about(own_key, extent, scale, most, shards=(), kind=jnp.bfloat16):
    entries = scale * jax.random.normal(own_key, extent, jnp.float32)
    if shards:
        entries = entries * level_of(own_key, extent, shards, -0.22, 0.18)
    return jnp.clip(entries, -most, most).astype(kind)


def setup_inputs(seed: int = 0) -> dict:
    key_list = jax.random.split(jax.random.key(seed), 7)
    query_proj = scatter_about(key_list[0], (SEQUENCE_STEPS, CH), 1.0, 6.0, ((0, 32), (1, 4)))
    key_proj = scatter_about(key_list[1], (SEQUENCE_STEPS, CH), 1.0, 6.0, ((0, 32), (1, 4)))
    value_proj = scatter_about(key_list[2], (SEQUENCE_STEPS, CH), 1.0, 6.0, ((0, 32), (1, 4)))
    filter_taps = draw_filter_taps(jax.random.fold_in(key_list[6], 71), 0)
    skip_gain = jnp.clip(jnp.exp(math.log(3.0) - 2.3025851 * jax.random.uniform(key_list[4], (CH,), jnp.float32) ** level_of(key_list[4], (CH,), ((0, 4),), -0.2, 0.2)), 0.3, 3.0)
    grad_mixer = scatter_about(key_list[5], (SEQUENCE_STEPS, CH), 1.0, 6.0, ((0, 32), (1, 4)))
    return {"query_proj": query_proj, "key_proj": key_proj, "value_proj": value_proj, "filter_taps": filter_taps, "skip_gain": skip_gain, "grad_mixer": grad_mixer}


def causal_conv(taps, signal):
    length = 2 * SEQUENCE_STEPS
    taps_hat = jnp.fft.rfft(taps, n=length, axis=0)
    signal_hat = jnp.fft.rfft(signal, n=length, axis=0)
    return jnp.fft.irfft(taps_hat * signal_hat, n=length, axis=0)[:SEQUENCE_STEPS]


def correlate(first, second):
    length = 2 * SEQUENCE_STEPS
    first_hat = jnp.fft.rfft(first, n=length, axis=0)
    second_hat = jnp.fft.rfft(second, n=length, axis=0)
    return jnp.fft.irfft(jnp.conj(first_hat) * second_hat, n=length, axis=0)[:SEQUENCE_STEPS]


def reference(query_proj, key_proj, value_proj, filter_taps, skip_gain, grad_mixer):
    repeats = CH // KERNEL_GROUPS
    taps_full = jnp.tile(filter_taps, (1, repeats))
    query = query_proj.astype(jnp.float32)
    key_data = key_proj.astype(jnp.float32)
    value_data = value_proj.astype(jnp.float32)
    upstream = grad_mixer.astype(jnp.float32)
    mixed = key_data * value_data
    conv = causal_conv(taps_full, mixed)
    pre = conv + skip_gain[None, :] * mixed
    mixer_out = (query * pre).astype(jnp.bfloat16)
    grad_in = upstream * query
    grad_query = (upstream * pre).astype(jnp.bfloat16)
    back = correlate(taps_full, grad_in) + skip_gain[None, :] * grad_in
    grad_key = (back * value_data).astype(jnp.bfloat16)
    grad_value = (back * key_data).astype(jnp.bfloat16)
    per_channel = correlate(mixed, grad_in)
    grad_filter = per_channel.reshape(SEQUENCE_STEPS, repeats, KERNEL_GROUPS).sum(axis=1) * (SEQUENCE_STEPS ** -0.5)
    return mixer_out, grad_query, grad_key, grad_value, grad_filter
```

```python
import functools
import math

import jax
import jax.numpy as jnp
import numpy as np
from jax import lax
from jax.experimental import pallas as pl
from jax.experimental.pallas import tpu as pltpu
from jax.sharding import PartitionSpec as P

FINE = 128
F32 = jnp.float32
BF16 = jnp.bfloat16


def split_table(table):
    high = table.astype(BF16)
    low = (table - high.astype(np.float64)).astype(BF16)
    return high, low


@functools.lru_cache(maxsize=None)
def tables(seq_count, pieces):
    coarse = seq_count * pieces
    total = coarse * FINE
    order = (pieces * np.arange(seq_count)[None, :] + np.arange(pieces)[:, None]).reshape(-1)
    low = np.arange(coarse) + 0.5
    fine = np.arange(FINE)
    angle = -2.0 * np.pi * low[:, None] * order[None, :] / (2 * coarse)
    first = np.concatenate([np.cos(angle), np.sin(angle)], axis=0)
    first_high, first_low = split_table(first)
    first_cat = np.concatenate([first_high, first_low, first_high], axis=1)
    last_high, last_low = split_table(first.T / total)
    turn = -2.0 * np.pi * low[:, None] * fine[None, :] / (2 * total)
    twist = np.stack([np.cos(turn), np.sin(turn)]).astype(np.float32)
    wave = -2.0 * np.pi * ((fine[:, None] * fine[None, :]) % FINE) / FINE
    re, im = np.cos(wave), np.sin(wave)
    forward = np.stack(split_table(np.block([[re, im], [-im, re]])))
    inverse = np.stack(split_table(np.block([[re, -im], [im, re]])))
    return first_cat, np.stack([last_high, last_low]), twist, forward, inverse


def dot(left, right):
    return jnp.dot(left, right, preferred_element_type=F32)


def halves(value):
    high = value.astype(BF16)
    return high, (value - high.astype(F32)).astype(BF16)


def pack_kernel(pieces, rows_per, query, key, value, grad, taps, out):
    own = lax.axis_index("ch")
    count = out.shape[0] // rows_per
    for piece in range(pieces):
        rows = pl.ds(FINE * piece, FINE)
        mixed = key[rows, :].astype(F32) * value[rows, :].astype(F32)
        grad_in = grad[rows, :].astype(F32) * query[rows, :].astype(F32)
        out[pl.ds(piece, count, stride=rows_per), :] = mixed.T
        out[pl.ds(pieces + piece, count, stride=rows_per), :] = grad_in.T
    rows = pl.ds(pl.multiple_of(own * FINE, FINE), FINE)
    out[pl.ds(2 * pieces, count, stride=rows_per), :] = taps[rows, :].T


def mix_kernel(
    seq_count, pieces, rows_in, rows_out,
    data, first, last, twist, forward, inverse,
    out, part_high, part_low, spec, back_high, back_low,
):
    groups = pieces
    coarse = seq_count * pieces
    signals = 2 * groups + 1

    def gather(start, step):
        return jnp.concatenate(
            [data[pl.ds(start + step * piece, seq_count, stride=rows_in), :] for piece in range(pieces)],
            axis=0,
        )

    def load(index):
        if index == 2 * groups:
            return gather(2 * pieces, seq_count * rows_in)
        group, kind = index % groups, index // groups
        return gather(group * seq_count * rows_in + kind * pieces, 1)

    twist_re, twist_im = twist[0], twist[1]
    for begin in range(0, signals, 2):
        members = range(begin, min(begin + 2, signals))
        high, low = halves(jnp.concatenate([load(i) for i in members], axis=1))
        mid = dot(first[...], jnp.concatenate([high, high, low], axis=0))
        for place, index in enumerate(members):
            cols = slice(FINE * place, FINE * place + FINE)
            re, im = mid[:coarse, cols], mid[coarse:, cols]
            turned_re = re * twist_re - im * twist_im
            turned_im = re * twist_im + im * twist_re
            rows = slice(coarse * index, coarse * index + coarse)
            part_high[rows, :FINE], part_low[rows, :FINE] = halves(turned_re)
            part_high[rows, FINE:], part_low[rows, FINE:] = halves(turned_im)

    spec[...] = (
        dot(part_high[...], forward[0]) + dot(part_low[...], forward[0]) + dot(part_high[...], forward[1])
    )

    def spectrum(index):
        rows = slice(coarse * index, coarse * index + coarse)
        return spec[rows, :FINE], spec[rows, FINE:]

    def keep(index, re, im):
        rows = slice(coarse * index, coarse * index + coarse)
        part_high[rows, :FINE], part_low[rows, :FINE] = halves(re)
        part_high[rows, FINE:], part_low[rows, FINE:] = halves(im)

    taps_re, taps_im = spectrum(2 * groups)
    corr_re = jnp.zeros_like(taps_re)
    corr_im = jnp.zeros_like(taps_im)
    for group in range(groups):
        mixed_re, mixed_im = spectrum(group)
        grad_re, grad_im = spectrum(groups + group)
        keep(group, taps_re * mixed_re - taps_im * mixed_im, taps_re * mixed_im + taps_im * mixed_re)
        keep(groups + group, taps_re * grad_re + taps_im * grad_im, taps_re * grad_im - taps_im * grad_re)
        corr_re += mixed_re * grad_re + mixed_im * grad_im
        corr_im += mixed_re * grad_im - mixed_im * grad_re
    keep(2 * groups, corr_re, corr_im)

    spec[...] = (
        dot(part_high[...], inverse[0]) + dot(part_low[...], inverse[0]) + dot(part_high[...], inverse[1])
    )
    for index in range(signals):
        re, im = spectrum(index)
        cols = slice(FINE * index, FINE * index + FINE)
        back_high[:coarse, cols], back_low[:coarse, cols] = halves(re * twist_re + im * twist_im)
        back_high[coarse:, cols], back_low[coarse:, cols] = halves(im * twist_re - re * twist_im)

    for index in range(signals):
        cols = slice(FINE * index, FINE * index + FINE)
        result = (
            dot(last[0], back_high[:, cols]) + dot(last[0], back_low[:, cols]) + dot(last[1], back_high[:, cols])
        )
        for piece in range(pieces):
            block = result[seq_count * piece : seq_count * piece + seq_count, :]
            if index == 2 * groups:
                for group in range(groups):
                    start = group * seq_count * rows_out + 2 * pieces + piece
                    out[pl.ds(start, seq_count, stride=rows_out), :] = block
            else:
                group, kind = index % groups, index // groups
                start = group * seq_count * rows_out + kind * pieces + piece
                out[pl.ds(start, seq_count, stride=rows_out), :] = block


def unpack_kernel(
    pieces, rows_per, scale, data, query, key, value, grad, gain,
    mixer_out, grad_query, grad_key, grad_value, grad_filter,
):
    own = lax.axis_index("ch")
    count = data.shape[0] // rows_per
    owned = grad_filter.shape[0]
    gain_row = gain[...]
    for piece in range(pieces):
        rows = pl.ds(FINE * piece, FINE)
        query_data, key_data = query[rows, :].astype(F32), key[rows, :].astype(F32)
        value_data, upstream = value[rows, :].astype(F32), grad[rows, :].astype(F32)
        conv = data[pl.ds(piece, count, stride=rows_per), :].T
        pre = conv + gain_row * (key_data * value_data)
        mixer_out[rows, :] = (query_data * pre).astype(BF16)
        grad_query[rows, :] = (upstream * pre).astype(BF16)
        corr = data[pl.ds(pieces + piece, count, stride=rows_per), :].T
        back = corr + gain_row * (upstream * query_data)
        grad_key[rows, :] = (back * value_data).astype(BF16)
        grad_value[rows, :] = (back * key_data).astype(BF16)
        start = own * (owned * rows_per) + 2 * pieces + piece
        grad_filter[:, rows] = data[pl.ds(start, owned, stride=rows_per), :] * scale


def local(query_proj, key_proj, value_proj, filter_taps, skip_gain, grad_mixer):
    seq_count = lax.axis_size("seq")
    ch_count = lax.axis_size("ch")
    devices = seq_count * ch_count
    local_rows, local_ch = query_proj.shape
    pieces = local_rows // FINE
    groups = ch_count
    assert devices == local_ch and pieces == groups
    rows_in = 2 * pieces + 1
    rows_out = 3 * pieces
    seq_total = local_rows * seq_count
    coarse = seq_count * pieces
    signals = 2 * groups + 1

    packed = pl.pallas_call(
        functools.partial(pack_kernel, pieces, rows_in),
        out_shape=jax.ShapeDtypeStruct((devices * rows_in, FINE), F32),
        compiler_params=pltpu.CompilerParams(vmem_limit_bytes=8 << 20),
        name="pack",
    )(query_proj, key_proj, value_proj, grad_mixer, filter_taps)

    def exchange(array, rows):
        array = array.reshape(devices, rows, 1, FINE)
        array = lax.all_to_all(array, ("ch", "seq"), 0, 0, tiled=True)
        return array.reshape(devices * rows, FINE)

    gathered = exchange(packed, rows_in)
    constants = [jnp.asarray(table) for table in tables(seq_count, pieces)]
    mixed = pl.pallas_call(
        functools.partial(mix_kernel, seq_count, pieces, rows_in, rows_out),
        out_shape=jax.ShapeDtypeStruct((devices * rows_out, FINE), F32),
        scratch_shapes=[
            pltpu.VMEM((signals * coarse, 2 * FINE), BF16),
            pltpu.VMEM((signals * coarse, 2 * FINE), BF16),
            pltpu.VMEM((signals * coarse, 2 * FINE), F32),
            pltpu.VMEM((2 * coarse, signals * FINE), BF16),
            pltpu.VMEM((2 * coarse, signals * FINE), BF16),
        ],
        compiler_params=pltpu.CompilerParams(vmem_limit_bytes=24 << 20),
        name="mix",
    )(gathered, *constants)
    returned = exchange(mixed, rows_out)

    out_bf16 = jax.ShapeDtypeStruct((local_rows, local_ch), BF16)
    *results, grad_filter = pl.pallas_call(
        functools.partial(unpack_kernel, pieces, rows_out, 1.0 / math.sqrt(seq_total)),
        out_shape=(
            out_bf16, out_bf16, out_bf16, out_bf16,
            jax.ShapeDtypeStruct((local_ch // ch_count, local_rows), F32),
        ),
        compiler_params=pltpu.CompilerParams(vmem_limit_bytes=8 << 20),
        name="unpack",
    )(returned, query_proj, key_proj, value_proj, grad_mixer, skip_gain[None, :])
    return (*results, grad_filter.T)


def solution(mesh):
    in_specs = (
        P("seq", "ch"),
        P("seq", "ch"),
        P("seq", "ch"),
        P("seq", None),
        P("ch"),
        P("seq", "ch"),
    )
    out_specs = (P("seq", "ch"), P("seq", "ch"), P("seq", "ch"), P("seq", "ch"), P("seq", "ch"))
    return jax.shard_map(local, mesh=mesh, in_specs=in_specs, out_specs=out_specs, check_vma=False)
```

```python
import functools
import math

import jax
import jax.numpy as jnp
import numpy as np
from jax import lax
from jax.experimental import pallas as pl
from jax.experimental.pallas import tpu as pltpu
from jax.sharding import PartitionSpec as P

FINE = 128
F32 = jnp.float32
BF16 = jnp.bfloat16


def split_table(table):
    high = table.astype(BF16)
    low = (table - high.astype(np.float64)).astype(BF16)
    return high, low


@functools.lru_cache(maxsize=None)
def tables(seq_count, pieces):
    coarse = seq_count * pieces
    total = coarse * FINE
    order = (pieces * np.arange(seq_count)[None, :] + np.arange(pieces)[:, None]).reshape(-1)
    low = np.arange(coarse) + 0.5
    fine = np.arange(FINE)
    angle = -2.0 * np.pi * low[:, None] * order[None, :] / (2 * coarse)
    first = np.concatenate([np.cos(angle), np.sin(angle)], axis=0)
    first_high, first_low = split_table(first)
    first_cat = np.concatenate([first_high, first_low, first_high], axis=1)
    last_high, last_low = split_table(first.T / total)
    turn = -2.0 * np.pi * low[:, None] * fine[None, :] / (2 * total)
    twist = np.stack([np.cos(turn), np.sin(turn)]).astype(np.float32)
    wave = -2.0 * np.pi * ((fine[:, None] * fine[None, :]) % FINE) / FINE
    re, im = np.cos(wave), np.sin(wave)
    forward = np.stack(split_table(np.block([[re, im], [-im, re]])))
    inverse = np.stack(split_table(np.block([[re, -im], [im, re]])))
    return first_cat, np.stack([last_high, last_low]), twist, forward, inverse


def dot(left, right):
    return jnp.dot(left, right, preferred_element_type=F32)


def halves(value):
    high = value.astype(BF16)
    return high, (value - high.astype(F32)).astype(BF16)


def pack_kernel(pieces, rows_per, query, key, value, grad, taps, gain, out, gain_out, *scratch):
    query_in, key_in, value_in, grad_in, taps_in, sems = scratch
    own = lax.axis_index("ch")
    count = out.shape[0] // rows_per
    rows = pl.ds(pl.multiple_of(own * FINE, FINE), FINE)
    taps_copy = pltpu.make_async_copy(taps.at[rows, :], taps_in, sems.at[4])
    gain_copy = pltpu.make_async_copy(gain, gain_out, sems.at[5])
    pairs = ((key, key_in), (value, value_in), (grad, grad_in), (query, query_in))
    copies = [pltpu.make_async_copy(src, dst, sems.at[i]) for i, (src, dst) in enumerate(pairs)]
    taps_copy.start()
    for copy in copies:
        copy.start()
    gain_copy.start()
    taps_copy.wait()
    out[pl.ds(2 * pieces, count, stride=rows_per), :] = taps_in[...].T
    copies[0].wait()
    copies[1].wait()
    for piece in range(pieces):
        rows = pl.ds(FINE * piece, FINE)
        mixed = key_in[rows, :].astype(F32) * value_in[rows, :].astype(F32)
        out[pl.ds(piece, count, stride=rows_per), :] = mixed.T
    copies[2].wait()
    copies[3].wait()
    for piece in range(pieces):
        rows = pl.ds(FINE * piece, FINE)
        grads = grad_in[rows, :].astype(F32) * query_in[rows, :].astype(F32)
        out[pl.ds(pieces + piece, count, stride=rows_per), :] = grads.T
    gain_copy.wait()


def mix_kernel(
    seq_count, pieces, rows_in, rows_out,
    data, first, last, twist, forward, inverse,
    out, part_high, part_low, spec, back_high, back_low,
):
    groups = pieces
    coarse = seq_count * pieces
    signals = 2 * groups + 1

    def gather(start, step):
        return jnp.concatenate(
            [data[pl.ds(start + step * piece, seq_count, stride=rows_in), :] for piece in range(pieces)],
            axis=0,
        )

    def load(index):
        if index == 2 * groups:
            return gather(2 * pieces, seq_count * rows_in)
        group, kind = index % groups, index // groups
        return gather(group * seq_count * rows_in + kind * pieces, 1)

    twist_re, twist_im = twist[0], twist[1]
    for begin in range(0, signals, 2):
        members = range(begin, min(begin + 2, signals))
        high, low = halves(jnp.concatenate([load(i) for i in members], axis=1))
        mid = dot(first[...], jnp.concatenate([high, high, low], axis=0))
        for place, index in enumerate(members):
            cols = slice(FINE * place, FINE * place + FINE)
            re, im = mid[:coarse, cols], mid[coarse:, cols]
            turned_re = re * twist_re - im * twist_im
            turned_im = re * twist_im + im * twist_re
            rows = slice(coarse * index, coarse * index + coarse)
            part_high[rows, :FINE], part_low[rows, :FINE] = halves(turned_re)
            part_high[rows, FINE:], part_low[rows, FINE:] = halves(turned_im)

    spec[...] = (
        dot(part_high[...], forward[0]) + dot(part_low[...], forward[0]) + dot(part_high[...], forward[1])
    )

    def spectrum(index):
        rows = slice(coarse * index, coarse * index + coarse)
        return spec[rows, :FINE], spec[rows, FINE:]

    def keep(index, re, im):
        rows = slice(coarse * index, coarse * index + coarse)
        part_high[rows, :FINE], part_low[rows, :FINE] = halves(re)
        part_high[rows, FINE:], part_low[rows, FINE:] = halves(im)

    taps_re, taps_im = spectrum(2 * groups)
    corr_re = jnp.zeros_like(taps_re)
    corr_im = jnp.zeros_like(taps_im)
    for group in range(groups):
        mixed_re, mixed_im = spectrum(group)
        grad_re, grad_im = spectrum(groups + group)
        keep(group, taps_re * mixed_re - taps_im * mixed_im, taps_re * mixed_im + taps_im * mixed_re)
        keep(groups + group, taps_re * grad_re + taps_im * grad_im, taps_re * grad_im - taps_im * grad_re)
        corr_re += mixed_re * grad_re + mixed_im * grad_im
        corr_im += mixed_re * grad_im - mixed_im * grad_re
    keep(2 * groups, corr_re, corr_im)

    spec[...] = (
        dot(part_high[...], inverse[0]) + dot(part_low[...], inverse[0]) + dot(part_high[...], inverse[1])
    )
    for index in range(signals):
        re, im = spectrum(index)
        cols = slice(FINE * index, FINE * index + FINE)
        back_high[:coarse, cols], back_low[:coarse, cols] = halves(re * twist_re + im * twist_im)
        back_high[coarse:, cols], back_low[coarse:, cols] = halves(im * twist_re - re * twist_im)

    for index in range(signals):
        cols = slice(FINE * index, FINE * index + FINE)
        result = (
            dot(last[0], back_high[:, cols]) + dot(last[0], back_low[:, cols]) + dot(last[1], back_high[:, cols])
        )
        for piece in range(pieces):
            block = result[seq_count * piece : seq_count * piece + seq_count, :]
            if index == 2 * groups:
                for group in range(groups):
                    start = group * seq_count * rows_out + 2 * pieces + piece
                    out[pl.ds(start, seq_count, stride=rows_out), :] = block
            else:
                group, kind = index % groups, index // groups
                start = group * seq_count * rows_out + kind * pieces + piece
                out[pl.ds(start, seq_count, stride=rows_out), :] = block


def unpack_kernel(
    pieces, rows_per, scale, data, query, key, value, grad, gain,
    mixer_out, grad_query, grad_key, grad_value, grad_filter, *scratch,
):
    holds, filter_hold, sems = scratch[:4], scratch[4], scratch[5]
    own = lax.axis_index("ch")
    count = data.shape[0] // rows_per
    owned = grad_filter.shape[0]
    gain_row = gain[...]
    copies = []

    def send(index, piece, target):
        rows = pl.ds(FINE * piece, FINE)
        copy = pltpu.make_async_copy(holds[index].at[rows, :], target.at[rows, :], sems.at[index, piece])
        copy.start()
        copies.append(copy)

    for piece in range(pieces):
        start = own * (owned * rows_per) + 2 * pieces + piece
        filter_hold[:, FINE * piece : FINE * piece + FINE] = data[pl.ds(start, owned, stride=rows_per), :] * scale
    filter_copy = pltpu.make_async_copy(filter_hold, grad_filter, sems.at[4, 0])
    filter_copy.start()
    for piece in range(pieces):
        rows = pl.ds(FINE * piece, FINE)
        query_data, key_data = query[rows, :].astype(F32), key[rows, :].astype(F32)
        value_data, upstream = value[rows, :].astype(F32), grad[rows, :].astype(F32)
        conv = data[pl.ds(piece, count, stride=rows_per), :].T
        pre = conv + gain_row * (key_data * value_data)
        holds[0][rows, :] = (query_data * pre).astype(BF16)
        send(0, piece, mixer_out)
        holds[1][rows, :] = (upstream * pre).astype(BF16)
        send(1, piece, grad_query)
        corr = data[pl.ds(pieces + piece, count, stride=rows_per), :].T
        back = corr + gain_row * (upstream * query_data)
        holds[2][rows, :] = (back * value_data).astype(BF16)
        send(2, piece, grad_key)
        holds[3][rows, :] = (back * key_data).astype(BF16)
        send(3, piece, grad_value)
    filter_copy.wait()
    for copy in copies:
        copy.wait()


def local(query_proj, key_proj, value_proj, filter_taps, skip_gain, grad_mixer):
    seq_count = lax.axis_size("seq")
    ch_count = lax.axis_size("ch")
    devices = seq_count * ch_count
    local_rows, local_ch = query_proj.shape
    pieces = local_rows // FINE
    groups = ch_count
    assert devices == local_ch and pieces == groups
    rows_in = 2 * pieces + 1
    rows_out = 3 * pieces
    seq_total = local_rows * seq_count
    coarse = seq_count * pieces
    signals = 2 * groups + 1

    hbm = pl.BlockSpec(memory_space=pltpu.HBM)
    vmem = pl.BlockSpec(memory_space=pltpu.VMEM)
    half = pltpu.VMEM((local_rows, local_ch), BF16)
    packed, gain_row = pl.pallas_call(
        functools.partial(pack_kernel, pieces, rows_in),
        out_shape=(
            jax.ShapeDtypeStruct((devices * rows_in, FINE), F32),
            jax.ShapeDtypeStruct((1, local_ch), F32),
        ),
        in_specs=[hbm] * 6,
        out_specs=(vmem, vmem),
        scratch_shapes=[half] * 4 + [pltpu.VMEM((FINE, local_ch), F32), pltpu.SemaphoreType.DMA((6,))],
        compiler_params=pltpu.CompilerParams(vmem_limit_bytes=8 << 20),
        name="pack",
    )(*[pltpu.with_memory_space_constraint(x, pltpu.HBM) for x in (query_proj, key_proj, value_proj, grad_mixer, filter_taps, skip_gain[None, :])])

    def exchange(array, rows):
        array = array.reshape(devices, rows, 1, FINE)
        array = lax.all_to_all(array, ("ch", "seq"), 0, 0, tiled=True)
        return array.reshape(devices * rows, FINE)

    gathered = exchange(packed, rows_in)
    constants = [jnp.asarray(table) for table in tables(seq_count, pieces)]
    mixed = pl.pallas_call(
        functools.partial(mix_kernel, seq_count, pieces, rows_in, rows_out),
        out_shape=jax.ShapeDtypeStruct((devices * rows_out, FINE), F32),
        scratch_shapes=[
            pltpu.VMEM((signals * coarse, 2 * FINE), BF16),
            pltpu.VMEM((signals * coarse, 2 * FINE), BF16),
            pltpu.VMEM((signals * coarse, 2 * FINE), F32),
            pltpu.VMEM((2 * coarse, signals * FINE), BF16),
            pltpu.VMEM((2 * coarse, signals * FINE), BF16),
        ],
        compiler_params=pltpu.CompilerParams(vmem_limit_bytes=24 << 20),
        name="mix",
    )(gathered, *constants)
    returned = exchange(mixed, rows_out)

    out_bf16 = jax.ShapeDtypeStruct((local_rows, local_ch), BF16)
    *results, grad_filter = pl.pallas_call(
        functools.partial(unpack_kernel, pieces, rows_out, 1.0 / math.sqrt(seq_total)),
        out_shape=(
            out_bf16, out_bf16, out_bf16, out_bf16,
            jax.ShapeDtypeStruct((local_ch // ch_count, local_rows), F32),
        ),
        in_specs=[vmem] * 6,
        out_specs=(hbm,) * 5,
        scratch_shapes=[half] * 4
        + [pltpu.VMEM((local_ch // ch_count, local_rows), F32), pltpu.SemaphoreType.DMA((5, pieces))],
        compiler_params=pltpu.CompilerParams(vmem_limit_bytes=8 << 20),
        name="unpack",
    )(returned, query_proj, key_proj, value_proj, grad_mixer, gain_row)
    return (*results, grad_filter.T)


def solution(mesh):
    in_specs = (
        P("seq", "ch"),
        P("seq", "ch"),
        P("seq", "ch"),
        P("seq", None),
        P("ch"),
        P("seq", "ch"),
    )
    out_specs = (P("seq", "ch"), P("seq", "ch"), P("seq", "ch"), P("seq", "ch"), P("seq", "ch"))
    return jax.shard_map(local, mesh=mesh, in_specs=in_specs, out_specs=out_specs, check_vma=False)
```

```python
import functools
import math

import jax
import jax.numpy as jnp
import numpy as np
from jax import lax
from jax.experimental import pallas as pl
from jax.experimental.pallas import tpu as pltpu
from jax.sharding import PartitionSpec as P

FINE = 128
F32 = jnp.float32
BF16 = jnp.bfloat16


def split_table(table):
    high = table.astype(BF16)
    low = (table - high.astype(np.float64)).astype(BF16)
    return high, low


def stacked(pair):
    high, low = pair
    return np.concatenate([high, high, low], axis=0)


@functools.lru_cache(maxsize=None)
def tables(seq_count, pieces):
    coarse = seq_count * pieces
    total = coarse * FINE
    order = (pieces * np.arange(seq_count)[None, :] + np.arange(pieces)[:, None]).reshape(-1)
    low = np.arange(coarse) + 0.5
    fine = np.arange(FINE)
    angle = -2.0 * np.pi * low[:, None] * order[None, :] / (2 * coarse)
    first = np.concatenate([np.cos(angle), np.sin(angle)], axis=0)
    first_high, first_low = split_table(first)
    first_cat = np.concatenate([first_high, first_low, first_high], axis=1)
    last_high, last_low = split_table(first.T / total)
    turn = -2.0 * np.pi * low[:, None] * fine[None, :] / (2 * total)
    twist = np.stack([np.cos(turn), np.sin(turn)]).astype(np.float32)
    wave = -2.0 * np.pi * ((fine[:, None] * fine[None, :]) % FINE) / FINE
    re, im = np.cos(wave), np.sin(wave)
    stack = [stacked(split_table(np.block(parts))) for parts in ([[re, im], [-im, re]], [[re, -im], [im, re]])]
    last_cat = np.concatenate([last_high, last_low], axis=0)
    return first_cat, last_cat, twist, *stack


def dot(left, right):
    return jnp.dot(left, right, preferred_element_type=F32)


def halves(value):
    high = value.astype(BF16)
    return high, (value - high.astype(F32)).astype(BF16)


def pack_kernel(pieces, rows_per, query, key, value, grad, taps, gain, out, gain_out, *scratch):
    query_in, key_in, value_in, grad_in, taps_in, sems = scratch
    own = lax.axis_index("ch")
    count = out.shape[0] // rows_per
    rows = pl.ds(pl.multiple_of(own * FINE, FINE), FINE)
    taps_copy = pltpu.make_async_copy(taps.at[rows, :], taps_in, sems.at[4])
    gain_copy = pltpu.make_async_copy(gain, gain_out, sems.at[5])
    pairs = ((key, key_in), (value, value_in), (grad, grad_in), (query, query_in))
    copies = [pltpu.make_async_copy(src, dst, sems.at[i]) for i, (src, dst) in enumerate(pairs)]
    taps_copy.start()
    for copy in copies:
        copy.start()
    gain_copy.start()
    taps_copy.wait()
    out[pl.ds(2 * pieces, count, stride=rows_per), :] = taps_in[...].T
    copies[0].wait()
    copies[1].wait()
    for piece in range(pieces):
        rows = pl.ds(FINE * piece, FINE)
        mixed = key_in[rows, :].astype(F32) * value_in[rows, :].astype(F32)
        out[pl.ds(piece, count, stride=rows_per), :] = mixed.T
    copies[2].wait()
    copies[3].wait()
    for piece in range(pieces):
        rows = pl.ds(FINE * piece, FINE)
        grads = grad_in[rows, :].astype(F32) * query_in[rows, :].astype(F32)
        out[pl.ds(pieces + piece, count, stride=rows_per), :] = grads.T
    gain_copy.wait()


def mix_kernel(
    seq_count, pieces, rows_in, rows_out, data, first, last, twist, forward, inverse, out,
):
    groups = pieces
    coarse = seq_count * pieces

    def gather(start, step):
        return jnp.concatenate(
            [data[pl.ds(start + step * piece, seq_count, stride=rows_in), :] for piece in range(pieces)],
            axis=0,
        )

    def turn(re, im, sign):
        turn_re, turn_im = twist[0], twist[1] * sign if sign < 0 else twist[1]
        return re * turn_re - im * turn_im, re * turn_im + im * turn_re

    def wave(parts, table):
        pairs = [halves(jnp.concatenate(part, axis=1)) for part in parts]
        high = jnp.concatenate([pair[0] for pair in pairs], axis=0)
        low = jnp.concatenate([pair[1] for pair in pairs], axis=0)
        count = high.shape[0]
        both = dot(jnp.concatenate([high, low], axis=0), table[: 2 * FINE, :])
        product = both[:count] + (both[count:] + dot(high, table[4 * FINE :, :]))
        return [
            (product[coarse * i : coarse * i + coarse, :FINE], product[coarse * i : coarse * i + coarse, FINE:])
            for i in range(len(parts))
        ]

    def begin(signals):
        high, low = halves(jnp.concatenate(signals, axis=1))
        return dot(first[...], jnp.concatenate([high, high, low], axis=0))

    def twisted(mid):
        parts = []
        for i in range(mid.shape[1] // FINE):
            cols = slice(FINE * i, FINE * i + FINE)
            parts.append(turn(mid[:coarse, cols], mid[coarse:, cols], 1))
        return parts

    def multiply(spectra):
        (mixed_re, mixed_im), (grad_re, grad_im) = spectra
        conv = (taps_re * mixed_re - taps_im * mixed_im, taps_re * mixed_im + taps_im * mixed_re)
        back = (taps_re * grad_re + taps_im * grad_im, taps_re * grad_im - taps_im * grad_re)
        corr = (mixed_re * grad_re + mixed_im * grad_im, mixed_re * grad_im - mixed_im * grad_re)
        return conv, back, corr

    def untwist(spectra):
        return [turn(re, im, -1) for re, im in spectra]

    def finish(parts):
        pairs = [halves(jnp.concatenate(part, axis=0)) for part in parts]
        high = jnp.concatenate([pair[0] for pair in pairs], axis=1)
        low = jnp.concatenate([pair[1] for pair in pairs], axis=1)
        both = dot(last[...], high)
        result = both[:coarse] + (both[coarse:] + dot(last[:coarse, :], low))
        return [result[:, FINE * i : FINE * i + FINE] for i in range(len(parts))]

    def put(block, group, row):
        for piece in range(pieces):
            start = group * seq_count * rows_out + row + piece
            out[pl.ds(start, seq_count, stride=rows_out), :] = block[
                seq_count * piece : seq_count * piece + seq_count, :
            ]

    keys = ["t", *range(groups)]
    load = {key: ([gather(2 * pieces, seq_count * rows_in)] if key == "t" else [gather(key * seq_count * rows_in, 1), gather(key * seq_count * rows_in + pieces, 1)]) for key in keys}
    mids = {key: begin(load[key]) for key in keys}
    parts = {key: twisted(mids[key]) for key in keys}
    spectra = {key: wave(parts[key], forward) for key in keys}
    ((taps_re, taps_im),) = spectra["t"]
    products = {group: multiply(spectra[group]) for group in range(groups)}
    corr = tuple(sum(products[group][2][part] for group in range(groups)) for part in range(2))
    lists = {group: list(products[group][:2]) for group in range(groups)}
    lists["t"] = [corr]
    order = [*range(groups), "t"]
    waves = {key: wave(lists[key], inverse) for key in order}
    turned = {key: untwist(waves[key]) for key in order}
    results = {key: finish(turned[key]) for key in order}
    for group in range(groups):
        for kind, block in enumerate(results[group]):
            put(block, group, kind * pieces)
        put(results["t"][0], group, 2 * pieces)


def unpack_kernel(
    pieces, rows_per, scale, data, query, key, value, grad, gain,
    mixer_out, grad_query, grad_key, grad_value, grad_filter, *scratch,
):
    holds, filter_hold, sems = scratch[:4], scratch[4], scratch[5]
    own = lax.axis_index("ch")
    count = data.shape[0] // rows_per
    owned = grad_filter.shape[0]
    gain_row = gain[...]
    copies = []

    def send(index, piece, target):
        rows = pl.ds(FINE * piece, FINE)
        copy = pltpu.make_async_copy(holds[index].at[rows, :], target.at[rows, :], sems.at[index, piece])
        copy.start()
        copies.append(copy)

    for piece in range(pieces):
        start = own * (owned * rows_per) + 2 * pieces + piece
        filter_hold[:, FINE * piece : FINE * piece + FINE] = data[pl.ds(start, owned, stride=rows_per), :] * scale
    filter_copy = pltpu.make_async_copy(filter_hold, grad_filter, sems.at[4, 0])
    filter_copy.start()
    for piece in range(pieces):
        rows = pl.ds(FINE * piece, FINE)
        query_data, key_data = query[rows, :].astype(F32), key[rows, :].astype(F32)
        value_data, upstream = value[rows, :].astype(F32), grad[rows, :].astype(F32)
        conv = data[pl.ds(piece, count, stride=rows_per), :].T
        pre = conv + gain_row * (key_data * value_data)
        holds[0][rows, :] = (query_data * pre).astype(BF16)
        send(0, piece, mixer_out)
        holds[1][rows, :] = (upstream * pre).astype(BF16)
        send(1, piece, grad_query)
        corr = data[pl.ds(pieces + piece, count, stride=rows_per), :].T
        back = corr + gain_row * (upstream * query_data)
        holds[2][rows, :] = (back * value_data).astype(BF16)
        send(2, piece, grad_key)
        holds[3][rows, :] = (back * key_data).astype(BF16)
        send(3, piece, grad_value)
    filter_copy.wait()
    for copy in copies:
        copy.wait()


def local(query_proj, key_proj, value_proj, filter_taps, skip_gain, grad_mixer):
    seq_count = lax.axis_size("seq")
    ch_count = lax.axis_size("ch")
    devices = seq_count * ch_count
    local_rows, local_ch = query_proj.shape
    pieces = local_rows // FINE
    groups = ch_count
    assert devices == local_ch and pieces == groups
    rows_in = 2 * pieces + 1
    rows_out = 3 * pieces
    seq_total = local_rows * seq_count

    hbm = pl.BlockSpec(memory_space=pltpu.HBM)
    vmem = pl.BlockSpec(memory_space=pltpu.VMEM)
    half = pltpu.VMEM((local_rows, local_ch), BF16)
    packed, gain_row = pl.pallas_call(
        functools.partial(pack_kernel, pieces, rows_in),
        out_shape=(
            jax.ShapeDtypeStruct((devices * rows_in, FINE), F32),
            jax.ShapeDtypeStruct((1, local_ch), F32),
        ),
        in_specs=[hbm] * 6,
        out_specs=(vmem, vmem),
        scratch_shapes=[half] * 4 + [pltpu.VMEM((FINE, local_ch), F32), pltpu.SemaphoreType.DMA((6,))],
        compiler_params=pltpu.CompilerParams(vmem_limit_bytes=8 << 20),
        name="pack",
    )(*[pltpu.with_memory_space_constraint(x, pltpu.HBM) for x in (query_proj, key_proj, value_proj, grad_mixer, filter_taps, skip_gain[None, :])])

    def exchange(array, rows):
        array = array.reshape(devices, rows, 1, FINE)
        array = lax.all_to_all(array, ("ch", "seq"), 0, 0, tiled=True)
        return array.reshape(devices * rows, FINE)

    gathered = exchange(packed, rows_in)
    constants = [jnp.asarray(table) for table in tables(seq_count, pieces)]
    mixed = pl.pallas_call(
        functools.partial(mix_kernel, seq_count, pieces, rows_in, rows_out),
        out_shape=jax.ShapeDtypeStruct((devices * rows_out, FINE), F32),
        compiler_params=pltpu.CompilerParams(vmem_limit_bytes=24 << 20),
        name="mix",
    )(gathered, *constants)
    returned = exchange(mixed, rows_out)

    out_bf16 = jax.ShapeDtypeStruct((local_rows, local_ch), BF16)
    *results, grad_filter = pl.pallas_call(
        functools.partial(unpack_kernel, pieces, rows_out, 1.0 / math.sqrt(seq_total)),
        out_shape=(
            out_bf16, out_bf16, out_bf16, out_bf16,
            jax.ShapeDtypeStruct((local_ch // ch_count, local_rows), F32),
        ),
        in_specs=[vmem] * 6,
        out_specs=(hbm,) * 5,
        scratch_shapes=[half] * 4
        + [pltpu.VMEM((local_ch // ch_count, local_rows), F32), pltpu.SemaphoreType.DMA((5, pieces))],
        compiler_params=pltpu.CompilerParams(vmem_limit_bytes=8 << 20),
        name="unpack",
    )(returned, query_proj, key_proj, value_proj, grad_mixer, gain_row)
    return (*results, grad_filter.T)


def solution(mesh):
    in_specs = (
        P("seq", "ch"),
        P("seq", "ch"),
        P("seq", "ch"),
        P("seq", None),
        P("ch"),
        P("seq", "ch"),
    )
    out_specs = (P("seq", "ch"), P("seq", "ch"), P("seq", "ch"), P("seq", "ch"), P("seq", "ch"))
    return jax.shard_map(local, mesh=mesh, in_specs=in_specs, out_specs=out_specs, check_vma=False)
```

```python
import functools
import math

import jax
import jax.numpy as jnp
import numpy as np
from jax import lax
from jax.experimental import pallas as pl
from jax.experimental.pallas import tpu as pltpu
from jax.sharding import PartitionSpec as P

FINE = 128
F32 = jnp.float32
BF16 = jnp.bfloat16


def split_table(table):
    high = table.astype(BF16)
    low = (table - high.astype(np.float64)).astype(BF16)
    return high, low


def stacked(pair):
    high, low = pair
    return np.concatenate([high, high, low], axis=0)


@functools.lru_cache(maxsize=None)
def tables(seq_count, pieces):
    coarse = seq_count * pieces
    total = coarse * FINE
    order = (pieces * np.arange(seq_count)[None, :] + np.arange(pieces)[:, None]).reshape(-1)
    low = np.arange(coarse) + 0.5
    fine = np.arange(FINE)
    angle = -2.0 * np.pi * low[:, None] * order[None, :] / (2 * coarse)
    first = np.concatenate([np.cos(angle), np.sin(angle)], axis=0)
    first_high, first_low = split_table(first)
    first_cat = np.concatenate([first_high, first_low, first_high], axis=1)
    last_high, last_low = split_table(first.T / total)
    turn = -2.0 * np.pi * low[:, None] * fine[None, :] / (2 * total)
    twist = np.stack([np.cos(turn), np.sin(turn)]).astype(np.float32)
    wave = -2.0 * np.pi * ((fine[:, None] * fine[None, :]) % FINE) / FINE
    re, im = np.cos(wave), np.sin(wave)
    stack = [stacked(split_table(np.block(parts))) for parts in ([[re, im], [-im, re]], [[re, -im], [im, re]])]
    last_cat = np.concatenate([last_high, last_low], axis=0)
    return first_cat, last_cat, twist, *stack


def dot(left, right):
    return jnp.dot(left, right, preferred_element_type=F32)


def halves(value):
    high = value.astype(BF16)
    return high, (value - high.astype(F32)).astype(BF16)


def pack_kernel(pieces, rows_per, query, key, value, grad, taps, out, *scratch):
    query_in, key_in, value_in, grad_in, taps_in, sems = scratch
    own = lax.axis_index("ch")
    count = out.shape[0] // rows_per
    rows = pl.ds(pl.multiple_of(own * FINE, FINE), FINE)
    taps_copy = pltpu.make_async_copy(taps.at[rows, :], taps_in, sems.at[4])
    pairs = ((key, key_in), (value, value_in), (grad, grad_in), (query, query_in))
    copies = [pltpu.make_async_copy(src, dst, sems.at[i]) for i, (src, dst) in enumerate(pairs)]
    taps_copy.start()
    for copy in copies:
        copy.start()
    taps_copy.wait()
    out[pl.ds(2 * pieces, count, stride=rows_per), :] = taps_in[...].T
    copies[0].wait()
    copies[1].wait()
    for piece in range(pieces):
        rows = pl.ds(FINE * piece, FINE)
        mixed = key_in[rows, :].astype(F32) * value_in[rows, :].astype(F32)
        out[pl.ds(piece, count, stride=rows_per), :] = mixed.T
    copies[2].wait()
    copies[3].wait()
    for piece in range(pieces):
        rows = pl.ds(FINE * piece, FINE)
        grads = grad_in[rows, :].astype(F32) * query_in[rows, :].astype(F32)
        out[pl.ds(pieces + piece, count, stride=rows_per), :] = grads.T


def mix_kernel(
    seq_count, pieces, rows_in, rows_out, data, first, last, twist, forward, inverse, gain, out, gain_out, gain_sem,
):
    groups = pieces
    coarse = seq_count * pieces
    gain_copy = pltpu.make_async_copy(gain, gain_out, gain_sem)
    gain_copy.start()

    def gather(start, step):
        return jnp.concatenate(
            [data[pl.ds(start + step * piece, seq_count, stride=rows_in), :] for piece in range(pieces)],
            axis=0,
        )

    def turn(re, im, sign):
        turn_re, turn_im = twist[0], twist[1] * sign if sign < 0 else twist[1]
        return re * turn_re - im * turn_im, re * turn_im + im * turn_re

    def wave(parts, table):
        pairs = [halves(jnp.concatenate(part, axis=1)) for part in parts]
        high = jnp.concatenate([pair[0] for pair in pairs], axis=0)
        low = jnp.concatenate([pair[1] for pair in pairs], axis=0)
        count = high.shape[0]
        both = dot(jnp.concatenate([high, low], axis=0), table[: 2 * FINE, :])
        product = both[:count] + (both[count:] + dot(high, table[4 * FINE :, :]))
        return [
            (product[coarse * i : coarse * i + coarse, :FINE], product[coarse * i : coarse * i + coarse, FINE:])
            for i in range(len(parts))
        ]

    def begin(signals):
        high, low = halves(jnp.concatenate(signals, axis=1))
        return dot(first[...], jnp.concatenate([high, high, low], axis=0))

    def twisted(mid):
        parts = []
        for i in range(mid.shape[1] // FINE):
            cols = slice(FINE * i, FINE * i + FINE)
            parts.append(turn(mid[:coarse, cols], mid[coarse:, cols], 1))
        return parts

    def multiply(spectra):
        (mixed_re, mixed_im), (grad_re, grad_im) = spectra
        conv = (taps_re * mixed_re - taps_im * mixed_im, taps_re * mixed_im + taps_im * mixed_re)
        back = (taps_re * grad_re + taps_im * grad_im, taps_re * grad_im - taps_im * grad_re)
        corr = (mixed_re * grad_re + mixed_im * grad_im, mixed_re * grad_im - mixed_im * grad_re)
        return conv, back, corr

    def untwist(spectra):
        return [turn(re, im, -1) for re, im in spectra]

    def finish(parts):
        pairs = [halves(jnp.concatenate(part, axis=0)) for part in parts]
        high = jnp.concatenate([pair[0] for pair in pairs], axis=1)
        low = jnp.concatenate([pair[1] for pair in pairs], axis=1)
        both = dot(last[...], high)
        result = both[:coarse] + (both[coarse:] + dot(last[:coarse, :], low))
        return [result[:, FINE * i : FINE * i + FINE] for i in range(len(parts))]

    def put(block, group, row):
        for piece in range(pieces):
            start = group * seq_count * rows_out + row + piece
            out[pl.ds(start, seq_count, stride=rows_out), :] = block[
                seq_count * piece : seq_count * piece + seq_count, :
            ]

    keys = ["t", *range(groups)]
    load = {key: ([gather(2 * pieces, seq_count * rows_in)] if key == "t" else [gather(key * seq_count * rows_in, 1), gather(key * seq_count * rows_in + pieces, 1)]) for key in keys}
    mids = {key: begin(load[key]) for key in keys}
    parts = {key: twisted(mids[key]) for key in keys}
    spectra = {key: wave(parts[key], forward) for key in keys}
    ((taps_re, taps_im),) = spectra["t"]
    products = {group: multiply(spectra[group]) for group in range(groups)}
    corr = tuple(sum(products[group][2][part] for group in range(groups)) for part in range(2))
    lists = {group: list(products[group][:2]) for group in range(groups)}
    lists["t"] = [corr]
    order = [*range(groups), "t"]
    waves = {key: wave(lists[key], inverse) for key in order}
    turned = {key: untwist(waves[key]) for key in order}
    results = {key: finish(turned[key]) for key in order}
    for group in range(groups):
        for kind, block in enumerate(results[group]):
            put(block, group, kind * pieces)
        put(results["t"][0], group, 2 * pieces)
    gain_copy.wait()


def unpack_kernel(
    pieces, rows_per, scale, data, query, key, value, grad, gain,
    mixer_out, grad_query, grad_key, grad_value, grad_filter, *scratch,
):
    holds, filter_hold, sems = scratch[:4], scratch[4], scratch[5]
    own = lax.axis_index("ch")
    count = data.shape[0] // rows_per
    owned = grad_filter.shape[0]
    gain_row = gain[...]
    targets = (mixer_out, grad_query, grad_key, grad_value)
    copies = [pltpu.make_async_copy(holds[i], targets[i], sems.at[i]) for i in range(4)]
    copies.append(pltpu.make_async_copy(filter_hold, grad_filter, sems.at[4]))
    for piece in range(pieces):
        rows = pl.ds(FINE * piece, FINE)
        mixed = key[rows, :].astype(F32) * value[rows, :].astype(F32)
        conv = data[pl.ds(piece, count, stride=rows_per), :].T
        pre = conv + gain_row * mixed
        holds[0][rows, :] = (query[rows, :].astype(F32) * pre).astype(BF16)
        holds[1][rows, :] = (grad[rows, :].astype(F32) * pre).astype(BF16)
    copies[0].start()
    copies[1].start()
    for piece in range(pieces):
        rows = pl.ds(FINE * piece, FINE)
        upstream = grad[rows, :].astype(F32) * query[rows, :].astype(F32)
        corr = data[pl.ds(pieces + piece, count, stride=rows_per), :].T
        back = corr + gain_row * upstream
        holds[2][rows, :] = (back * value[rows, :].astype(F32)).astype(BF16)
        holds[3][rows, :] = (back * key[rows, :].astype(F32)).astype(BF16)
    copies[2].start()
    copies[3].start()
    for piece in range(pieces):
        start = own * (owned * rows_per) + 2 * pieces + piece
        filter_hold[:, FINE * piece : FINE * piece + FINE] = data[pl.ds(start, owned, stride=rows_per), :] * scale
    copies[4].start()
    for copy in copies:
        copy.wait()


def local(query_proj, key_proj, value_proj, filter_taps, skip_gain, grad_mixer):
    seq_count = lax.axis_size("seq")
    ch_count = lax.axis_size("ch")
    devices = seq_count * ch_count
    local_rows, local_ch = query_proj.shape
    pieces = local_rows // FINE
    groups = ch_count
    assert devices == local_ch and pieces == groups
    rows_in = 2 * pieces + 1
    rows_out = 3 * pieces
    seq_total = local_rows * seq_count

    hbm = pl.BlockSpec(memory_space=pltpu.HBM)
    vmem = pl.BlockSpec(memory_space=pltpu.VMEM)
    half = pltpu.VMEM((local_rows, local_ch), BF16)
    packed = pl.pallas_call(
        functools.partial(pack_kernel, pieces, rows_in),
        out_shape=jax.ShapeDtypeStruct((devices * rows_in, FINE), F32),
        in_specs=[hbm] * 5,
        out_specs=vmem,
        scratch_shapes=[half] * 4 + [pltpu.VMEM((FINE, local_ch), F32), pltpu.SemaphoreType.DMA((5,))],
        compiler_params=pltpu.CompilerParams(vmem_limit_bytes=8 << 20),
        name="pack",
    )(*[pltpu.with_memory_space_constraint(x, pltpu.HBM) for x in (query_proj, key_proj, value_proj, grad_mixer, filter_taps)])

    def exchange(array, rows):
        array = array.reshape(devices, rows, 1, FINE)
        array = lax.all_to_all(array, ("ch", "seq"), 0, 0, tiled=True)
        return array.reshape(devices * rows, FINE)

    gathered = exchange(packed, rows_in)
    constants = [jnp.asarray(table) for table in tables(seq_count, pieces)]
    mixed, gain_row = pl.pallas_call(
        functools.partial(mix_kernel, seq_count, pieces, rows_in, rows_out),
        out_shape=(
            jax.ShapeDtypeStruct((devices * rows_out, FINE), F32),
            jax.ShapeDtypeStruct((1, local_ch), F32),
        ),
        in_specs=[vmem] * 6 + [hbm],
        out_specs=(vmem, vmem),
        scratch_shapes=[pltpu.SemaphoreType.DMA],
        compiler_params=pltpu.CompilerParams(vmem_limit_bytes=24 << 20),
        name="mix",
    )(gathered, *constants, pltpu.with_memory_space_constraint(skip_gain[None, :], pltpu.HBM))
    returned = exchange(mixed, rows_out)

    out_bf16 = jax.ShapeDtypeStruct((local_rows, local_ch), BF16)
    *results, grad_filter = pl.pallas_call(
        functools.partial(unpack_kernel, pieces, rows_out, 1.0 / math.sqrt(seq_total)),
        out_shape=(
            out_bf16, out_bf16, out_bf16, out_bf16,
            jax.ShapeDtypeStruct((local_ch // ch_count, local_rows), F32),
        ),
        in_specs=[vmem] * 6,
        out_specs=(hbm,) * 5,
        scratch_shapes=[half] * 4
        + [pltpu.VMEM((local_ch // ch_count, local_rows), F32), pltpu.SemaphoreType.DMA((5,))],
        compiler_params=pltpu.CompilerParams(vmem_limit_bytes=8 << 20),
        name="unpack",
    )(returned, query_proj, key_proj, value_proj, grad_mixer, gain_row)
    return (*results, grad_filter.T)


def solution(mesh):
    in_specs = (
        P("seq", "ch"),
        P("seq", "ch"),
        P("seq", "ch"),
        P("seq", None),
        P("ch"),
        P("seq", "ch"),
    )
    out_specs = (P("seq", "ch"), P("seq", "ch"), P("seq", "ch"), P("seq", "ch"), P("seq", "ch"))
    return jax.shard_map(local, mesh=mesh, in_specs=in_specs, out_specs=out_specs, check_vma=False)
```

```python
import functools
import math

import jax
import jax.numpy as jnp
import numpy as np
from jax import lax
from jax.experimental import pallas as pl
from jax.experimental.pallas import tpu as pltpu
from jax.sharding import PartitionSpec as P

FINE = 128
F32 = jnp.float32
BF16 = jnp.bfloat16


def split_table(table):
    high = table.astype(BF16)
    low = (table - high.astype(np.float64)).astype(BF16)
    return high, low


def stacked(pair):
    high, low = pair
    return np.concatenate([high, high, low], axis=0)


@functools.lru_cache(maxsize=None)
def tables(seq_count, pieces):
    coarse = seq_count * pieces
    total = coarse * FINE
    order = (pieces * np.arange(seq_count)[None, :] + np.arange(pieces)[:, None]).reshape(-1)
    low = np.concatenate([np.arange(coarse // 2), coarse - 1 - np.arange(coarse // 2)]) + 0.5
    fine = np.arange(FINE)
    angle = -2.0 * np.pi * low[:, None] * order[None, :] / (2 * coarse)
    first = np.concatenate([np.cos(angle), np.sin(angle)], axis=0)
    first_cat = []
    for parity in range(2):
        half = first[:, order % 2 == parity]
        half_high, half_low = split_table(np.concatenate([half[: coarse // 2], half[coarse : coarse + coarse // 2]]))
        first_cat.append(np.concatenate([half_high, half_low, half_high], axis=1))
    first_cat = np.stack(first_cat)
    last_high, last_low = split_table(first.T / total)
    turn = -2.0 * np.pi * low[:, None] * fine[None, :] / (2 * total)
    twist = np.stack([np.cos(turn), np.sin(turn)]).astype(np.float32)
    wave = -2.0 * np.pi * ((fine[:, None] * fine[None, :]) % FINE) / FINE
    re, im = np.cos(wave), np.sin(wave)
    stack = [stacked(split_table(np.block(parts))) for parts in ([[re, im], [-im, re]], [[re, -im], [im, re]])]
    last_cat = np.concatenate([last_high, last_low], axis=0)
    return first_cat, last_cat, twist, *stack


def dot(left, right):
    return jnp.dot(left, right, preferred_element_type=F32)


def halves(value):
    high = value.astype(BF16)
    return high, (value - high.astype(F32)).astype(BF16)


def pack_kernel(pieces, rows_per, query, key, value, grad, taps, out, *scratch):
    query_in, key_in, value_in, grad_in, taps_in, sems = scratch
    own = lax.axis_index("ch")
    count = out.shape[0] // rows_per
    rows = pl.ds(pl.multiple_of(own * FINE, FINE), FINE)
    taps_copy = pltpu.make_async_copy(taps.at[rows, :], taps_in, sems.at[4])
    pairs = ((key, key_in), (value, value_in), (grad, grad_in), (query, query_in))
    copies = [pltpu.make_async_copy(src, dst, sems.at[i]) for i, (src, dst) in enumerate(pairs)]
    taps_copy.start()
    for copy in copies:
        copy.start()
    taps_copy.wait()
    out[pl.ds(2 * pieces, count, stride=rows_per), :] = taps_in[...].T
    copies[0].wait()
    copies[1].wait()
    for piece in range(pieces):
        rows = pl.ds(FINE * piece, FINE)
        mixed = key_in[rows, :].astype(F32) * value_in[rows, :].astype(F32)
        out[pl.ds(piece, count, stride=rows_per), :] = mixed.T
    copies[2].wait()
    copies[3].wait()
    for piece in range(pieces):
        rows = pl.ds(FINE * piece, FINE)
        grads = grad_in[rows, :].astype(F32) * query_in[rows, :].astype(F32)
        out[pl.ds(pieces + piece, count, stride=rows_per), :] = grads.T


def mix_kernel(
    seq_count, pieces, rows_in, rows_out, data, first, last, twist, forward, inverse, gain, out, gain_out, gain_sem,
):
    groups = pieces
    coarse = seq_count * pieces
    gain_copy = pltpu.make_async_copy(gain, gain_out, gain_sem)
    gain_copy.start()

    def gather(start, step):
        return jnp.concatenate(
            [data[pl.ds(start + step * piece, seq_count, stride=rows_in), :] for piece in range(pieces)],
            axis=0,
        )

    def turn(re, im, sign):
        turn_re, turn_im = twist[0], twist[1] * sign if sign < 0 else twist[1]
        return re * turn_re - im * turn_im, re * turn_im + im * turn_re

    def wave(parts, table):
        pairs = [halves(jnp.concatenate(part, axis=1)) for part in parts]
        high = jnp.concatenate([pair[0] for pair in pairs], axis=0)
        low = jnp.concatenate([pair[1] for pair in pairs], axis=0)
        count = high.shape[0]
        both = dot(jnp.concatenate([high, low], axis=0), table[: 2 * FINE, :])
        product = both[:count] + (both[count:] + dot(high, table[4 * FINE :, :]))
        return [
            (product[coarse * i : coarse * i + coarse, :FINE], product[coarse * i : coarse * i + coarse, FINE:])
            for i in range(len(parts))
        ]

    def begin(signals):
        sums = []
        for parity in range(2):
            part = jnp.concatenate(
                [
                    jnp.concatenate(
                        [signal[seq_count * p : seq_count * p + seq_count] for p in range(parity, pieces, 2)], axis=0
                    )
                    for signal in signals
                ],
                axis=1,
            )
            high, low = halves(part)
            sums.append(dot(first[parity], jnp.concatenate([high, high, low], axis=0)))
        even, odd = sums
        mid = coarse // 2
        return jnp.concatenate(
            [even[:mid] + odd[:mid], even[:mid] - odd[:mid], even[mid:] + odd[mid:], odd[mid:] - even[mid:]], axis=0
        )

    def twisted(mid):
        parts = []
        for i in range(mid.shape[1] // FINE):
            cols = slice(FINE * i, FINE * i + FINE)
            parts.append(turn(mid[:coarse, cols], mid[coarse:, cols], 1))
        return parts

    def multiply(spectra):
        (mixed_re, mixed_im), (grad_re, grad_im) = spectra
        conv = (taps_re * mixed_re - taps_im * mixed_im, taps_re * mixed_im + taps_im * mixed_re)
        back = (taps_re * grad_re + taps_im * grad_im, taps_re * grad_im - taps_im * grad_re)
        corr = (mixed_re * grad_re + mixed_im * grad_im, mixed_re * grad_im - mixed_im * grad_re)
        return conv, back, corr

    def untwist(spectra):
        return [turn(re, im, -1) for re, im in spectra]

    def finish(parts):
        pairs = [halves(jnp.concatenate(part, axis=0)) for part in parts]
        high = jnp.concatenate([pair[0] for pair in pairs], axis=1)
        low = jnp.concatenate([pair[1] for pair in pairs], axis=1)
        both = dot(last[...], high)
        result = both[:coarse] + (both[coarse:] + dot(last[:coarse, :], low))
        return [result[:, FINE * i : FINE * i + FINE] for i in range(len(parts))]

    def put(block, group, row):
        for piece in range(pieces):
            start = group * seq_count * rows_out + row + piece
            out[pl.ds(start, seq_count, stride=rows_out), :] = block[
                seq_count * piece : seq_count * piece + seq_count, :
            ]

    keys = ["t", *range(groups)]
    load = {key: ([gather(2 * pieces, seq_count * rows_in)] if key == "t" else [gather(key * seq_count * rows_in, 1), gather(key * seq_count * rows_in + pieces, 1)]) for key in keys}
    mids = {key: begin(load[key]) for key in keys}
    parts = {key: twisted(mids[key]) for key in keys}
    spectra = {key: wave(parts[key], forward) for key in keys}
    ((taps_re, taps_im),) = spectra["t"]
    products = {group: multiply(spectra[group]) for group in range(groups)}
    corr = tuple(sum(products[group][2][part] for group in range(groups)) for part in range(2))
    lists = {group: list(products[group][:2]) for group in range(groups)}
    lists["t"] = [corr]
    order = [*range(groups), "t"]
    waves = {key: wave(lists[key], inverse) for key in order}
    turned = {key: untwist(waves[key]) for key in order}
    results = {key: finish(turned[key]) for key in order}
    for group in range(groups):
        for kind, block in enumerate(results[group]):
            put(block, group, kind * pieces)
        put(results["t"][0], group, 2 * pieces)
    gain_copy.wait()


def unpack_kernel(
    pieces, rows_per, scale, data, query, key, value, grad, gain,
    mixer_out, grad_query, grad_key, grad_value, grad_filter, *scratch,
):
    holds, filter_hold, sems = scratch[:4], scratch[4], scratch[5]
    own = lax.axis_index("ch")
    count = data.shape[0] // rows_per
    owned = grad_filter.shape[0]
    gain_row = gain[...]
    targets = (mixer_out, grad_query, grad_key, grad_value)
    copies = [pltpu.make_async_copy(holds[i], targets[i], sems.at[i]) for i in range(4)]
    copies.append(pltpu.make_async_copy(filter_hold, grad_filter, sems.at[4]))
    for piece in range(pieces):
        rows = pl.ds(FINE * piece, FINE)
        mixed = key[rows, :].astype(F32) * value[rows, :].astype(F32)
        conv = data[pl.ds(piece, count, stride=rows_per), :].T
        pre = conv + gain_row * mixed
        holds[0][rows, :] = (query[rows, :].astype(F32) * pre).astype(BF16)
        holds[1][rows, :] = (grad[rows, :].astype(F32) * pre).astype(BF16)
    copies[0].start()
    copies[1].start()
    for piece in range(pieces):
        rows = pl.ds(FINE * piece, FINE)
        upstream = grad[rows, :].astype(F32) * query[rows, :].astype(F32)
        corr = data[pl.ds(pieces + piece, count, stride=rows_per), :].T
        back = corr + gain_row * upstream
        holds[2][rows, :] = (back * value[rows, :].astype(F32)).astype(BF16)
        holds[3][rows, :] = (back * key[rows, :].astype(F32)).astype(BF16)
    copies[2].start()
    copies[3].start()
    for piece in range(pieces):
        start = own * (owned * rows_per) + 2 * pieces + piece
        filter_hold[:, FINE * piece : FINE * piece + FINE] = data[pl.ds(start, owned, stride=rows_per), :] * scale
    copies[4].start()
    for copy in copies:
        copy.wait()


def local(query_proj, key_proj, value_proj, filter_taps, skip_gain, grad_mixer):
    seq_count = lax.axis_size("seq")
    ch_count = lax.axis_size("ch")
    devices = seq_count * ch_count
    local_rows, local_ch = query_proj.shape
    pieces = local_rows // FINE
    groups = ch_count
    assert devices == local_ch and pieces == groups
    rows_in = 2 * pieces + 1
    rows_out = 3 * pieces
    seq_total = local_rows * seq_count

    hbm = pl.BlockSpec(memory_space=pltpu.HBM)
    vmem = pl.BlockSpec(memory_space=pltpu.VMEM)
    half = pltpu.VMEM((local_rows, local_ch), BF16)
    packed = pl.pallas_call(
        functools.partial(pack_kernel, pieces, rows_in),
        out_shape=jax.ShapeDtypeStruct((devices * rows_in, FINE), F32),
        in_specs=[hbm] * 5,
        out_specs=vmem,
        scratch_shapes=[half] * 4 + [pltpu.VMEM((FINE, local_ch), F32), pltpu.SemaphoreType.DMA((5,))],
        compiler_params=pltpu.CompilerParams(vmem_limit_bytes=8 << 20),
        name="pack",
    )(*[pltpu.with_memory_space_constraint(x, pltpu.HBM) for x in (query_proj, key_proj, value_proj, grad_mixer, filter_taps)])

    def exchange(array, rows):
        array = array.reshape(devices, rows, 1, FINE)
        array = lax.all_to_all(array, ("ch", "seq"), 0, 0, tiled=True)
        return array.reshape(devices * rows, FINE)

    gathered = exchange(packed, rows_in)
    constants = [jnp.asarray(table) for table in tables(seq_count, pieces)]
    mixed, gain_row = pl.pallas_call(
        functools.partial(mix_kernel, seq_count, pieces, rows_in, rows_out),
        out_shape=(
            jax.ShapeDtypeStruct((devices * rows_out, FINE), F32),
            jax.ShapeDtypeStruct((1, local_ch), F32),
        ),
        in_specs=[vmem] * 6 + [hbm],
        out_specs=(vmem, vmem),
        scratch_shapes=[pltpu.SemaphoreType.DMA],
        compiler_params=pltpu.CompilerParams(vmem_limit_bytes=24 << 20),
        name="mix",
    )(gathered, *constants, pltpu.with_memory_space_constraint(skip_gain[None, :], pltpu.HBM))
    returned = exchange(mixed, rows_out)

    out_bf16 = jax.ShapeDtypeStruct((local_rows, local_ch), BF16)
    *results, grad_filter = pl.pallas_call(
        functools.partial(unpack_kernel, pieces, rows_out, 1.0 / math.sqrt(seq_total)),
        out_shape=(
            out_bf16, out_bf16, out_bf16, out_bf16,
            jax.ShapeDtypeStruct((local_ch // ch_count, local_rows), F32),
        ),
        in_specs=[vmem] * 6,
        out_specs=(hbm,) * 5,
        scratch_shapes=[half] * 4
        + [pltpu.VMEM((local_ch // ch_count, local_rows), F32), pltpu.SemaphoreType.DMA((5,))],
        compiler_params=pltpu.CompilerParams(vmem_limit_bytes=8 << 20),
        name="unpack",
    )(returned, query_proj, key_proj, value_proj, grad_mixer, gain_row)
    return (*results, grad_filter.T)


def solution(mesh):
    in_specs = (
        P("seq", "ch"),
        P("seq", "ch"),
        P("seq", "ch"),
        P("seq", None),
        P("ch"),
        P("seq", "ch"),
    )
    out_specs = (P("seq", "ch"), P("seq", "ch"), P("seq", "ch"), P("seq", "ch"), P("seq", "ch"))
    return jax.shard_map(local, mesh=mesh, in_specs=in_specs, out_specs=out_specs, check_vma=False)
```
